256 devices in a mesh: dp: 8 (over x, core), expert: 32 (over z, y).
Axes of the slice: x: 4, y: 4, z: 8, core: 2. Of those that a mesh axis runs over, the one named last changes fastest.
Arguments:
- tokens: bfloat16 [2048, 3584], P(('dp', 'expert')), may hold values from -6 to 6
- cotangent: bfloat16 [2048, 3584], P(('dp', 'expert')), may hold values from -6 to 6
- routes: int32 [2048, 8], P(('dp', 'expert')), may hold values from 0 to 31, all different within a row; in each aligned block of 8 rows (0 to 7, 8 to 15, ...) at most 3 rows name the same one
- gates: bfloat16 [2048, 8], P(('dp', 'expert')), may hold values from 0.049804688 to 1
- w_gate: bfloat16 [32, 3584, 2048], P('expert', None, 'dp'), may hold values from -0.09375 to 0.09375
- w_up: bfloat16 [32, 3584, 2048], P('expert', None, 'dp'), may hold values from -0.09375 to 0.09375
- w_down: bfloat16 [32, 2048, 3584], P('expert', 'dp'), may hold values from -0.125 to 0.125
Outputs:
- grad_tokens: bfloat16 [2048, 3584], P(('dp', 'expert'))
- grad_gate: bfloat16 [32, 3584, 2048], P('expert', None, 'dp')
- grad_up: bfloat16 [32, 3584, 2048], P('expert', None, 'dp')
- grad_down: bfloat16 [32, 2048, 3584], P('expert', 'dp')
The draws below stay inside these ranges and needn't reach their ends.
Inputs may be any that keep to these rules, and one draw needn't show every extreme that they name: `routes`: each row names 8 different experts; among the rows of one device no expert is named more than 3 times, a bound that some block reaches.
All inputs are finite; a program needn't handle non-finite values.
Results may differ from the reference program's by a relative error of at most 0.01.
Values may be sent and summed in bfloat16 or wider, within the bound.
No kernel may reach another device: no remote copies, remote signals or barrier semaphores. Data moves between devices by JAX's collectives and lax.ppermute only.
A program may use at most 128 MiB of HBM per device.

```python
import math
import jax
import jax.numpy as jnp
import numpy as np
from jax import lax

D = 3584
FF = 2048
TOP = 8
TOK_DEV = 8
EXPERTS = 32
CAP = 3
TOKENS = 2048
N_DP = 8
N_EXPERT = 32


def block_levels(key, shape, cuts, low, largest):
    def one(dim, shards_of):
        draws = jax.random.uniform(jax.random.fold_in(jax.random.fold_in(key, 6), dim), (shards_of,), jnp.float32, low / len(cuts), largest / len(cuts))
        return jnp.repeat(jnp.exp(draws), shape[dim] // shards_of).reshape((-1,) + (1,) * (len(shape) - dim - 1))

    loudness = one(*cuts[0])
    for cut in cuts[1:]:
        loudness = loudness * one(*cut)
    return loudness


def assign_block(stream_key, own, number, rows, amount, top, limit, lean):
    order = jax.random.permutation(stream_key, amount)
    crowded, usual = load_shares(amount, rows * top, limit, lean, True), load_shares(amount, rows * top, limit, lean, False)
    places = jnp.arange(amount)

    def named(lengths, rotation):
        used = int((lengths > 0).sum())
        fixed = max(1, used // 4)
        shifted = fixed + (places - fixed + rotation * (used - fixed)) % max(1, amount - fixed)
        return jnp.zeros((amount,), jnp.int32).at[order[jnp.where(places < fixed, places, shifted)]].set(jnp.asarray(lengths, jnp.int32))

    lengths = jnp.where(number % 4 == 0, named(crowded, number // 4), named(usual, number - number // 4 - 1))
    mixed = jax.random.permutation(jax.random.fold_in(own, 3), amount)
    source_of, receiver = mixed[0:amount // 2 * 2:2], mixed[1:amount // 2 * 2:2]
    margin = jnp.minimum(lengths[source_of] - 1, limit - lengths[receiver]) // 2
    margin = jnp.where((source_of == order[0]) | (receiver == order[0]) | (lengths[receiver] == 0), 0, jnp.maximum(margin, 0))
    shifted = jax.random.randint(jax.random.fold_in(own, 4), (amount // 2,), 0, 1 << 20) % (margin + 1)
    lengths = lengths.at[source_of].add(-shifted).at[receiver].add(shifted)
    items = jnp.searchsorted(jnp.cumsum(lengths), jnp.arange(rows * top), side="right").astype(jnp.int32)
    listing = items.reshape(top, rows).T
    listing = listing[jax.random.permutation(jax.random.fold_in(own, 1), rows)]
    rotation = jax.random.randint(jax.random.fold_in(own, 2), (rows, 1), 0, top)
    return jnp.take_along_axis(listing, (jnp.arange(top)[None, :] + rotation) % top, axis=1)


def load_shares(amount, total, limit, slope, full):
    weights = [(1 << 20) // math.isqrt(rank ** slope) + 1 for rank in range(1, amount + 1)]
    largest = limit if full else min(limit, max(-(-total // amount), total * weights[0] // sum(weights)))
    least = 1 if total - largest >= amount - 1 else 0
    counts, spare = [largest] + [least] * (amount - 1), total - largest - least * (amount - 1)
    while spare > 0:
        movable = [i for i in range(1, amount) if counts[i] < largest] or [i for i in range(1, amount) if counts[i] < limit]
        pool, budget = sum([weights[i] for i in movable]), spare
        for i in movable:
            extra = min(limit - counts[i], max(1, budget * weights[i] // pool), spare)
            counts[i] = counts[i] + extra
            spare = spare - extra
    return np.array(counts)


def noise(key, dims, spread, reach, split=(), held_as=jnp.bfloat16):
    result = jax.random.normal(key, dims, jnp.float32) * spread
    if len(split) > 0:
        result = block_levels(key, dims, split, -0.22, 0.18) * result
    return jnp.clip(result, min=-reach, max=reach).astype(held_as)


def setup_inputs(seed: int = 0) -> dict:
    streams_of = jax.random.split(jax.random.key(seed), 8)
    tokens = noise(streams_of[0], (TOKENS, D), 1.0, 6.0, ((0, 256),))
    cotangent = noise(streams_of[1], (TOKENS, D), 1.0, 6.0, ((0, 256),))
    routes_keys = jax.random.split(jax.random.fold_in(streams_of[2], 1), TOKENS // TOK_DEV)
    routes_turns = jax.random.permutation(jax.random.fold_in(streams_of[2], 3), TOKENS // TOK_DEV)
    routes = jax.vmap(lambda own, number: assign_block(jax.random.fold_in(streams_of[2], 2), own, number, TOK_DEV, EXPERTS, TOP, CAP, 2))(routes_keys, routes_turns).reshape((TOKENS, TOP))
    gates = jnp.clip(jnp.exp(math.log(1.0) - 2.9996462 * jax.random.uniform(streams_of[3], (TOKENS, TOP), jnp.float32) ** block_levels(streams_of[3], (TOKENS, TOP), ((0, 256),), -0.2, 0.2)), 0.049804688, 1.0).astype(jnp.bfloat16)
    w_gate = noise(streams_of[4], (EXPERTS, D, FF), D ** -0.5, 0.09375, ((0, 32), (2, 8)))
    w_up = noise(streams_of[5], (EXPERTS, D, FF), D ** -0.5, 0.09375, ((0, 32), (2, 8)))
    w_down = noise(streams_of[6], (EXPERTS, FF, D), FF ** -0.5, 0.125, ((0, 32), (1, 8)))
    return dict(tokens=tokens, cotangent=cotangent, routes=routes, gates=gates, w_gate=w_gate, w_up=w_up, w_down=w_down)


def expert_terms(rows_x, rows_dy, gate_rows, gate_mat, up_mat, down_mat):
    gate_pre = jnp.dot(rows_x, gate_mat, preferred_element_type=jnp.float32)
    up_pre = jnp.dot(rows_x, up_mat, preferred_element_type=jnp.float32)
    sigmoid_g = jax.nn.sigmoid(gate_pre)
    activated = gate_pre * sigmoid_g
    gate_scale = gate_rows.astype(jnp.float32)[:, None]
    hidden = (gate_scale * activated * up_pre).astype(jnp.bfloat16)
    returned = gate_scale * jnp.dot(rows_dy, down_mat.T, preferred_element_type=jnp.float32)
    d_gate = (returned * up_pre * sigmoid_g * (1.0 + gate_pre * (1.0 - sigmoid_g))).astype(jnp.bfloat16)
    d_up = (returned * activated).astype(jnp.bfloat16)
    grad_gate = jnp.dot(rows_x.T, d_gate, preferred_element_type=jnp.float32)
    grad_up = jnp.dot(rows_x.T, d_up, preferred_element_type=jnp.float32)
    grad_down = jnp.dot(hidden.T, rows_dy, preferred_element_type=jnp.float32)
    return d_gate, d_up, grad_gate, grad_up, grad_down


def reference(tokens, cotangent, routes, gates, w_gate, w_up, w_down):
    dev_count = N_DP * N_EXPERT
    flat_ids = routes.reshape(dev_count, TOK_DEV * TOP)
    expert_iota = jnp.arange(EXPERTS, dtype=jnp.int32)
    onehot = (flat_ids[:, :, None] == expert_iota[None, None, :]).astype(jnp.int32)
    slot_pos = jnp.sum((jnp.cumsum(onehot, axis=1) - onehot) * onehot, axis=2).astype(jnp.int32)
    source = jnp.arange(dev_count, dtype=jnp.int32)[:, None]
    position = ((flat_ids * dev_count + source) * CAP + slot_pos).reshape(-1).astype(jnp.int32)
    token_of = (jnp.arange(TOKENS * TOP, dtype=jnp.int32) // TOP).astype(jnp.int32)
    slots_all = EXPERTS * dev_count * CAP
    row_table = jnp.full((slots_all,), TOKENS, jnp.int32).at[position].set(token_of)
    gate_table = jnp.zeros((slots_all,), jnp.float32).at[position].set(gates.reshape(-1).astype(jnp.float32))
    padded_x = jnp.concatenate([tokens, jnp.zeros((1, D), tokens.dtype)], axis=0)
    padded_dy = jnp.concatenate([cotangent, jnp.zeros((1, D), cotangent.dtype)], axis=0)

    def one_expert(carried, inputs):
        row_index, gate_rows, gate_mat, up_mat, down_mat = inputs
        rows_x = padded_x[row_index]
        rows_dy = padded_dy[row_index]
        d_gate, d_up, grad_gate, grad_up, grad_down = expert_terms(rows_x, rows_dy, gate_rows, gate_mat, up_mat, down_mat)
        partial_value = jnp.dot(d_gate, gate_mat.T, preferred_element_type=jnp.float32) + jnp.dot(d_up, up_mat.T, preferred_element_type=jnp.float32)
        return carried.at[row_index].add(partial_value), (grad_gate.astype(jnp.bfloat16), grad_up.astype(jnp.bfloat16), grad_down.astype(jnp.bfloat16))

    initial = jnp.zeros((TOKENS + 1, D), jnp.float32)
    total, grads = lax.scan(one_expert, initial, (row_table.reshape(EXPERTS, dev_count * CAP), gate_table.reshape(EXPERTS, dev_count * CAP), w_gate, w_up, w_down))
    return (total[:TOKENS].astype(jnp.bfloat16), grads[0], grads[1], grads[2])
```

```python
import functools

import jax
import jax.numpy as jnp
from jax import lax
from jax.experimental import pallas as pl
from jax.experimental.pallas import tpu as pltpu
from jax.sharding import PartitionSpec as P


BF = jnp.bfloat16
F32 = jnp.float32
LANES = 128
SLOTS = 3


def chunk_rows(tiles):
    return -(-SLOTS * tiles // 8) * 8


def deal(scratch, experts, tiles, value):
    chunk = chunk_rows(tiles)
    for j in range(SLOTS):
        for c in range(tiles):
            scratch[pl.ds(j * tiles + c, experts, stride=chunk), :] = value(
                slice(j * experts, (j + 1) * experts), slice(c * LANES, (c + 1) * LANES)
            )
    for n in range(SLOTS * tiles, chunk):
        scratch[pl.ds(n, experts, stride=chunk), :] = jnp.zeros((experts, LANES), F32)


def collect(scratch, experts, tiles, out):
    chunk = chunk_rows(tiles)
    for j in range(SLOTS):
        for c in range(tiles):
            out[j * experts : (j + 1) * experts, c * LANES : (c + 1) * LANES] = scratch[
                pl.ds(j * tiles + c, experts, stride=chunk), :
            ].astype(BF)


def pack_kernel(tok, cot, routes, gates, out_x, out_dy, pick, picked, scratch, *, experts):
    rows, features = tok.shape
    top = routes.shape[1]
    tiles = features // LANES
    lane = lax.broadcasted_iota(jnp.int32, (rows, LANES), 1)
    expert_of = lane % experts
    slot_of = lane // experts
    hit = jnp.zeros((rows, LANES), F32)
    gate = jnp.zeros((rows, LANES), F32)
    for k in range(top):
        same = routes[:, k : k + 1] == expert_of
        hit = jnp.where(same, 1.0, hit)
        gate = jnp.where(same, gates[:, k : k + 1].astype(F32), gate)
    below = lax.broadcasted_iota(jnp.int32, (rows, rows), 1) < lax.broadcasted_iota(jnp.int32, (rows, rows), 0)
    rank = jnp.dot(below.astype(BF), hit.astype(BF), preferred_element_type=F32)
    chosen = (hit > 0.5) & (rank == slot_of.astype(F32))
    sel = jnp.where(chosen, 1.0, 0.0)
    pick[...] = sel.astype(BF)

    def spread(mask, values):
        return lax.dot_general(mask.astype(BF), values, (((0,), (0,)), ((), ())), preferred_element_type=F32)

    picked[:, :features] = spread(sel, tok[...])
    deal(scratch, experts, tiles, lambda r, c: picked[r, c])
    out_x[...] = scratch[...].astype(BF)
    picked[:, :features] = spread(sel, cot[...])
    picked[:, features:] = spread(sel * gate, jnp.ones((rows, LANES), BF))
    deal(scratch, experts, tiles + 1, lambda r, c: picked[r, c])
    out_dy[...] = scratch[...].astype(BF)


def pack_rows(tokens, cotangent, routes, gates, experts):
    rows, features = tokens.shape
    tiles = features // LANES
    assert chunk_rows(tiles) == chunk_rows(tiles + 1)
    flat = (experts * chunk_rows(tiles), LANES)
    return pl.pallas_call(
        functools.partial(pack_kernel, experts=experts),
        out_shape=(
            jax.ShapeDtypeStruct(flat, BF),
            jax.ShapeDtypeStruct(flat, BF),
            jax.ShapeDtypeStruct((rows, LANES), BF),
        ),
        scratch_shapes=[pltpu.VMEM((LANES, features + LANES), F32), pltpu.VMEM(flat, F32)],
        name="pack_rows",
    )(tokens, cotangent, routes, gates)


def unpack_kernel(flat, out, scratch, *, experts):
    scratch[...] = flat[...].astype(F32)
    collect(scratch, experts, out.shape[1] // LANES, out)


def unpack_rows(flat, experts, width):
    return pl.pallas_call(
        functools.partial(unpack_kernel, experts=experts),
        out_shape=jax.ShapeDtypeStruct((SLOTS * experts, width), BF),
        scratch_shapes=[pltpu.VMEM(flat.shape, F32)],
        name="unpack_rows",
    )(flat)


def back_kernel(own, left, right, out, scratch, *, experts):
    deal(
        scratch,
        experts,
        own.shape[1] // LANES,
        lambda r, c: own[r, c].astype(F32) + left[r, c].astype(F32) + right[r, c].astype(F32),
    )
    out[...] = scratch[...].astype(BF)


def pack_back(own, left, right, experts):
    flat = (experts * chunk_rows(own.shape[1] // LANES), LANES)
    return pl.pallas_call(
        functools.partial(back_kernel, experts=experts),
        out_shape=jax.ShapeDtypeStruct(flat, BF),
        scratch_shapes=[pltpu.VMEM(flat, F32)],
        name="pack_back",
    )(own, left, right)


def combine_kernel(flat, pick, out, scratch, rows_ref, *, experts):
    scratch[...] = flat[...].astype(F32)
    collect(scratch, experts, out.shape[1] // LANES, rows_ref)
    out[...] = jnp.dot(pick[:, : SLOTS * experts], rows_ref[...], preferred_element_type=F32).astype(BF)


def combine_rows(flat, pick, experts, features):
    return pl.pallas_call(
        functools.partial(combine_kernel, experts=experts),
        out_shape=jax.ShapeDtypeStruct((pick.shape[0], features), BF),
        scratch_shapes=[pltpu.VMEM(flat.shape, F32), pltpu.VMEM((SLOTS * experts, features), BF)],
        name="combine_rows",
    )(flat, pick)


def weight_grads_kernel(*refs, xs, dys):
    refs = list(refs)
    take = lambda n: [refs.pop(0) for _ in range(n)]
    rows_x, rows_dy, hidden, d_gate, d_up = take(xs), take(dys), take(dys), take(dys), take(dys)
    out_gate, out_up, out_down = refs

    def product(a, b):
        a, b = (jnp.concatenate([piece[...] for piece in side], axis=0) for side in (a, b))
        return lax.dot_general(a, b, (((0,), (0,)), ((), ())), preferred_element_type=F32).astype(BF)

    out_gate[0] = product(rows_x, d_gate)
    out_up[0] = product(rows_x, d_up)
    out_down[0] = product(hidden, rows_dy)


def weight_grads(rows_x, rows_dy, terms, features):
    step = 512
    width = terms[0][0].shape[1]
    columns = tuple(zip(*terms))
    operands = [*rows_x, *rows_dy, *columns[0], *columns[1], *columns[2]]
    specs = [pl.BlockSpec((a.shape[0], step), lambda i: (0, i)) for a in (*rows_x, *rows_dy)]
    specs += [pl.BlockSpec(a.shape, lambda i: (0, 0)) for a in operands[len(specs) :]]
    tall = pl.BlockSpec((1, step, width), lambda i: (0, i, 0))
    return pl.pallas_call(
        functools.partial(weight_grads_kernel, xs=len(rows_x), dys=len(rows_dy)),
        grid=(features // step,),
        in_specs=specs,
        out_specs=(tall, tall, pl.BlockSpec((1, width, step), lambda i: (0, 0, i))),
        out_shape=(
            jax.ShapeDtypeStruct((1, features, width), BF),
            jax.ShapeDtypeStruct((1, features, width), BF),
            jax.ShapeDtypeStruct((1, width, features), BF),
        ),
        name="weight_grads",
    )(*operands)


def exchange(flat, experts):
    chunks = flat.reshape(experts, -1, LANES)
    out = lax.all_to_all(chunks, "expert", split_axis=0, concat_axis=0, tiled=True)
    return out.reshape(-1, LANES)


def shift(a, by, size):
    return lax.ppermute(a, "dp", [(i, (i + 2 * by) % size) for i in range(size)])


def swap(a, size):
    return lax.ppermute(a, "dp", [(i, i ^ 1) for i in range(size)])


def after(values, *others):
    return lax.optimization_barrier((tuple(values), others))[0] if others else tuple(values)


def relay(own, size):
    half = own.shape[0] // 2
    behind, ahead = shift(own, 1, size), shift(own, -1, size)
    return behind, ahead, shift(behind[:half], 1, size), shift(ahead[half:], -1, size)


def projections(rows, gate_mat, up_mat):
    gate_pre = jnp.dot(rows, gate_mat, preferred_element_type=F32)
    up_pre = jnp.dot(rows, up_mat, preferred_element_type=F32)
    return gate_pre, up_pre


def expert_terms(rows, gate_pre, up_pre, gate_mat, up_mat, down_mat):
    features = gate_mat.shape[0]
    weight = rows[:, features : features + 1].astype(F32)
    sig = jax.nn.sigmoid(gate_pre)
    activated = gate_pre * sig
    hidden = (weight * activated * up_pre).astype(BF)
    returned = weight * jnp.dot(rows[:, :features], down_mat.T, preferred_element_type=F32)
    d_gate = (returned * up_pre * sig * (1.0 + gate_pre * (1.0 - sig))).astype(BF)
    d_up = (returned * activated).astype(BF)
    total = jnp.dot(d_gate, gate_mat.T, preferred_element_type=F32) + jnp.dot(
        d_up, up_mat.T, preferred_element_type=F32
    )
    return total, (hidden, d_gate, d_up)


def per_device(tokens, cotangent, routes, gates, w_gate, w_up, w_down):
    features = tokens.shape[1]
    experts = lax.axis_size("expert")
    size = lax.axis_size("dp")
    mats = w_gate[0], w_up[0], w_down[0]
    flat_x, flat_dy, pick = pack_rows(tokens, cotangent, routes, gates, experts)
    own_x = unpack_rows(exchange(flat_x, experts), experts, features)
    (flat_dy,) = after((flat_dy,), own_x)
    own_dy = unpack_rows(exchange(flat_dy, experts), experts, features + LANES)
    rows = own_x.shape[0]
    half, near = rows // 2, 3 * rows
    behind, ahead, *far = relay(own_x, size)
    far = after(far, own_dy)
    mine_x = jnp.concatenate((own_x, behind, ahead, *far), axis=0)
    theirs_x = swap(mine_x, size)
    pre_m = projections(mine_x, *mats[:2])
    pre_t = projections(theirs_x, *mats[:2])
    behind, ahead = after((shift(own_dy, 1, size), shift(own_dy, -1, size)), *pre_m, *pre_t)
    halves = behind[:half], ahead[half:]
    far = shift(halves[0], 1, size), shift(halves[1], -1, size)
    near_m = jnp.concatenate(after((own_dy, behind, ahead), *halves), axis=0)
    total_nm, terms_nm = expert_terms(near_m, *(a[:near] for a in pre_m), *mats)
    (near_t,) = after((swap(near_m, size),), total_nm)
    total_nt, terms_nt = expert_terms(near_t, *(a[:near] for a in pre_t), *mats)
    swapped = swap(total_nt.astype(BF), size)
    far_m = jnp.concatenate(after(far, total_nt), axis=0)
    total_fm, terms_fm = expert_terms(far_m, *(a[near:] for a in pre_m), *mats)
    (far_t,) = after((swap(far_m, size),), total_fm)
    total_ft, terms_ft = expert_terms(far_t, *(a[near:] for a in pre_t), *mats)
    (total_ft,) = after((total_ft.astype(BF),), swapped)
    across = (total_fm + swap(total_ft, size).astype(F32)).astype(BF)
    total_n = total_nm + swapped.astype(F32)
    from_behind = shift(across[:half], 1, size).astype(F32)
    from_ahead = shift(across[half:], -1, size).astype(F32)
    own, behind, ahead = (total_n[k * rows : (k + 1) * rows] for k in range(3))
    ahead = jnp.concatenate((ahead[:half] + from_behind, ahead[half:]), axis=0).astype(BF)
    behind = jnp.concatenate((behind[:half], behind[half:] + from_ahead), axis=0).astype(BF)
    left, right = shift(ahead, 1, size), shift(behind, -1, size)
    back = exchange(pack_back(own.astype(BF), left, right, experts), experts)
    grad_x = combine_rows(back, pick, experts, features)
    grads = weight_grads(
        (mine_x, theirs_x), (near_m, far_m, near_t, far_t), (terms_nm, terms_fm, terms_nt, terms_ft), features
    )
    return (grad_x, *grads)


def solution(mesh):
    rows = P(("dp", "expert"), None)
    columns = P("expert", None, "dp")
    down = P("expert", "dp", None)
    return jax.shard_map(
        per_device,
        mesh=mesh,
        in_specs=(rows, rows, rows, rows, columns, columns, down),
        out_specs=(rows, columns, columns, down),
        check_vma=False,
    )
```

```python
import functools

import jax
import jax.numpy as jnp
from jax import lax
from jax.experimental import pallas as pl
from jax.experimental.pallas import tpu as pltpu
from jax.sharding import PartitionSpec as P


BF = jnp.bfloat16
F32 = jnp.float32
LANES = 128
SLOTS = 3


def held(a):
    return pltpu.with_memory_space_constraint(a, pltpu.VMEM)


def chunk_rows(tiles):
    return -(-SLOTS * tiles // 8) * 8


def deal(scratch, experts, tiles, value):
    chunk = chunk_rows(tiles)
    for j in range(SLOTS):
        for c in range(tiles):
            scratch[pl.ds(j * tiles + c, experts, stride=chunk), :] = value(
                slice(j * experts, (j + 1) * experts), slice(c * LANES, (c + 1) * LANES)
            )
    for n in range(SLOTS * tiles, chunk):
        scratch[pl.ds(n, experts, stride=chunk), :] = jnp.zeros((experts, LANES), F32)


def collect(scratch, experts, tiles, out):
    chunk = chunk_rows(tiles)
    for j in range(SLOTS):
        for c in range(tiles):
            out[j * experts : (j + 1) * experts, c * LANES : (c + 1) * LANES] = scratch[
                pl.ds(j * tiles + c, experts, stride=chunk), :
            ].astype(BF)


def pack_kernel(tok, cot, routes, gates, out_x, out_dy, pick, picked, scratch, *, experts):
    rows, features = tok.shape
    top = routes.shape[1]
    tiles = features // LANES
    lane = lax.broadcasted_iota(jnp.int32, (rows, LANES), 1)
    expert_of = lane % experts
    slot_of = lane // experts
    hit = jnp.zeros((rows, LANES), F32)
    gate = jnp.zeros((rows, LANES), F32)
    for k in range(top):
        same = routes[:, k : k + 1] == expert_of
        hit = jnp.where(same, 1.0, hit)
        gate = jnp.where(same, gates[:, k : k + 1].astype(F32), gate)
    below = lax.broadcasted_iota(jnp.int32, (rows, rows), 1) < lax.broadcasted_iota(jnp.int32, (rows, rows), 0)
    rank = jnp.dot(below.astype(BF), hit.astype(BF), preferred_element_type=F32)
    chosen = (hit > 0.5) & (rank == slot_of.astype(F32))
    sel = jnp.where(chosen, 1.0, 0.0)
    pick[...] = sel.astype(BF)

    def spread(mask, values):
        return lax.dot_general(mask.astype(BF), values, (((0,), (0,)), ((), ())), preferred_element_type=F32)

    picked[:, :features] = spread(sel, tok[...])
    deal(scratch, experts, tiles, lambda r, c: picked[r, c])
    out_x[...] = scratch[...].astype(BF)
    picked[:, :features] = spread(sel, cot[...])
    picked[:, features:] = spread(sel * gate, jnp.ones((rows, LANES), BF))
    deal(scratch, experts, tiles + 1, lambda r, c: picked[r, c])
    out_dy[...] = scratch[...].astype(BF)


def pack_rows(tokens, cotangent, routes, gates, experts):
    rows, features = tokens.shape
    tiles = features // LANES
    assert chunk_rows(tiles) == chunk_rows(tiles + 1)
    flat = (experts * chunk_rows(tiles), LANES)
    return pl.pallas_call(
        functools.partial(pack_kernel, experts=experts),
        out_shape=(
            jax.ShapeDtypeStruct(flat, BF),
            jax.ShapeDtypeStruct(flat, BF),
            jax.ShapeDtypeStruct((rows, LANES), BF),
        ),
        scratch_shapes=[pltpu.VMEM((LANES, features + LANES), F32), pltpu.VMEM(flat, F32)],
        name="pack_rows",
    )(tokens, cotangent, routes, gates)


def unpack_kernel(flat, out, scratch, *, experts):
    scratch[...] = flat[...].astype(F32)
    collect(scratch, experts, out.shape[1] // LANES, out)


def unpack_rows(flat, experts, width):
    return pl.pallas_call(
        functools.partial(unpack_kernel, experts=experts),
        out_shape=jax.ShapeDtypeStruct((SLOTS * experts, width), BF),
        scratch_shapes=[pltpu.VMEM(flat.shape, F32)],
        name="unpack_rows",
    )(held(flat))


def back_kernel(own, left_low, left_high, right_low, right_high, out, scratch, *, experts):
    half = own.shape[0] // 2

    def value(r, c):
        low, high = slice(r.start, min(r.stop, half)), slice(max(r.start, half) - half, r.stop - half)
        left, right = (
            jnp.concatenate([p[s, c] for p, s in ((a, low), (b, high)) if s.start < s.stop], axis=0).astype(F32)
            for a, b in ((left_low, left_high), (right_low, right_high))
        )
        return own[r, c].astype(F32) + left + right

    deal(scratch, experts, own.shape[1] // LANES, value)
    out[...] = scratch[...].astype(BF)


def pack_back(own, left_low, left_high, right_low, right_high, experts):
    flat = (experts * chunk_rows(own.shape[1] // LANES), LANES)
    return pl.pallas_call(
        functools.partial(back_kernel, experts=experts),
        out_shape=jax.ShapeDtypeStruct(flat, BF),
        scratch_shapes=[pltpu.VMEM(flat, F32)],
        name="pack_back",
    )(*(held(a) for a in (own, left_low, left_high, right_low, right_high)))


def combine_kernel(flat, pick, out, scratch, rows_ref, *, experts):
    scratch[...] = flat[...].astype(F32)
    collect(scratch, experts, out.shape[1] // LANES, rows_ref)
    out[...] = jnp.dot(pick[:, : SLOTS * experts], rows_ref[...], preferred_element_type=F32).astype(BF)


def combine_rows(flat, pick, experts, features):
    return pl.pallas_call(
        functools.partial(combine_kernel, experts=experts),
        out_shape=jax.ShapeDtypeStruct((pick.shape[0], features), BF),
        scratch_shapes=[pltpu.VMEM(flat.shape, F32), pltpu.VMEM((SLOTS * experts, features), BF)],
        name="combine_rows",
    )(held(flat), pick)


def weight_grads_kernel(*refs, xs, dys):
    refs = list(refs)
    take = lambda n: [refs.pop(0) for _ in range(n)]
    rows_x, rows_dy, hidden, d_gate, d_up = take(xs), take(dys), take(dys), take(dys), take(dys)
    out_gate, out_up, out_down = refs

    def product(a, b):
        a, b = (jnp.concatenate([piece[...] for piece in side], axis=0) for side in (a, b))
        return lax.dot_general(a, b, (((0,), (0,)), ((), ())), preferred_element_type=F32).astype(BF)

    out_gate[0] = product(rows_x, d_gate)
    out_up[0] = product(rows_x, d_up)
    out_down[0] = product(hidden, rows_dy)


def weight_grads(rows_x, rows_dy, terms, features):
    step = 512
    width = terms[0][0].shape[1]
    columns = tuple(zip(*terms))
    operands = [*rows_x, *rows_dy, *columns[0], *columns[1], *columns[2]]
    specs = [pl.BlockSpec((a.shape[0], step), lambda i: (0, i)) for a in (*rows_x, *rows_dy)]
    specs += [pl.BlockSpec(a.shape, lambda i: (0, 0)) for a in operands[len(specs) :]]
    tall = pl.BlockSpec((1, step, width), lambda i: (0, i, 0))
    return pl.pallas_call(
        functools.partial(weight_grads_kernel, xs=len(rows_x), dys=len(rows_dy)),
        grid=(features // step,),
        in_specs=specs,
        out_specs=(tall, tall, pl.BlockSpec((1, width, step), lambda i: (0, 0, i))),
        out_shape=(
            jax.ShapeDtypeStruct((1, features, width), BF),
            jax.ShapeDtypeStruct((1, features, width), BF),
            jax.ShapeDtypeStruct((1, width, features), BF),
        ),
        name="weight_grads",
    )(*operands)


def exchange(flat, experts):
    chunks = flat.reshape(experts, -1, LANES)
    out = lax.all_to_all(chunks, "expert", split_axis=0, concat_axis=0, tiled=True)
    return out.reshape(-1, LANES)


def shift(a, by, size):
    return lax.ppermute(a, "dp", [(i, (i + 2 * by) % size) for i in range(size)])


def swap(a, size):
    return lax.ppermute(a, "dp", [(i, i ^ 1) for i in range(size)])


def after(values, *others):
    return lax.optimization_barrier((tuple(values), others))[0] if others else tuple(values)


def projections(rows, gate_mat, up_mat):
    gate_pre = jnp.dot(rows, gate_mat, preferred_element_type=F32)
    up_pre = jnp.dot(rows, up_mat, preferred_element_type=F32)
    return gate_pre, up_pre


def expert_terms(rows, gate_pre, up_pre, gate_mat, up_mat, down_mat):
    features = gate_mat.shape[0]
    weight = rows[:, features : features + 1].astype(F32)
    sig = jax.nn.sigmoid(gate_pre)
    activated = gate_pre * sig
    hidden = (weight * activated * up_pre).astype(BF)
    returned = weight * jnp.dot(rows[:, :features], down_mat.T, preferred_element_type=F32)
    d_gate = (returned * up_pre * sig * (1.0 + gate_pre * (1.0 - sig))).astype(BF)
    d_up = (returned * activated).astype(BF)
    total = jnp.dot(d_gate, gate_mat.T, preferred_element_type=F32) + jnp.dot(
        d_up, up_mat.T, preferred_element_type=F32
    )
    return total, (hidden, d_gate, d_up)


def per_device(tokens, cotangent, routes, gates, w_gate, w_up, w_down):
    features = tokens.shape[1]
    experts = lax.axis_size("expert")
    size = lax.axis_size("dp")
    mats = w_gate[0], w_up[0], w_down[0]
    flat_x, flat_dy, pick = pack_rows(tokens, cotangent, routes, gates, experts)
    own_x = unpack_rows(exchange(flat_x, experts), experts, features)
    rows = own_x.shape[0]
    half = rows // 2
    behind, ahead = shift(own_x, 1, size), shift(own_x, -1, size)
    halves = behind[:half], ahead[half:]
    far = shift(halves[0], 1, size), shift(halves[1], -1, size)
    (flat_dy,) = after((exchange(flat_dy, experts),), *halves)
    own_dy = unpack_rows(flat_dy, experts, features + LANES)
    near_xm = jnp.concatenate(after((own_x, behind, ahead), own_dy), axis=0)
    near_xt = swap(near_xm, size)
    pre_nm = projections(near_xm, *mats[:2])
    pre_nt = projections(near_xt, *mats[:2])
    far_xm = jnp.concatenate(after(far, *pre_nm), axis=0)
    far_xt = swap(far_xm, size)
    pre_fm = projections(far_xm, *mats[:2])
    pre_ft = projections(far_xt, *mats[:2])
    sides = shift(own_dy, 1, size), shift(own_dy, -1, size)
    behind, ahead = after(sides, *pre_nt, *pre_fm, *pre_ft)
    halves = behind[:half], ahead[half:]
    far = shift(halves[0], 1, size), shift(halves[1], -1, size)
    near_m = jnp.concatenate(after((own_dy, behind, ahead), *halves), axis=0)
    near_t = swap(near_m, size)
    total_nm, terms_nm = expert_terms(near_m, *pre_nm, *mats)
    (near_t,) = after((near_t,), total_nm)
    total_nt, terms_nt = expert_terms(near_t, *pre_nt, *mats)
    swapped = swap(total_nt.astype(BF), size)
    far_m = jnp.concatenate(after(far, total_nt), axis=0)
    total_fm, terms_fm = expert_terms(far_m, *pre_fm, *mats)
    (far_t,) = after((swap(far_m, size),), total_fm)
    total_ft, terms_ft = expert_terms(far_t, *pre_ft, *mats)
    (total_ft,) = after((total_ft.astype(BF),), swapped)
    across = (total_fm + swap(total_ft, size).astype(F32)).astype(BF)
    total_n = total_nm + swapped.astype(F32)
    own, behind, ahead = (total_n[k * rows : (k + 1) * rows] for k in range(3))
    right_ready = shift(behind[:half].astype(BF), -1, size)
    left_ready = shift(ahead[half:].astype(BF), 1, size)
    from_behind = shift(across[:half], 1, size).astype(F32)
    from_ahead = shift(across[half:], -1, size).astype(F32)
    left_late = shift((ahead[:half] + from_behind).astype(BF), 1, size)
    right_late = shift((behind[half:] + from_ahead).astype(BF), -1, size)
    sides = left_late, left_ready, right_ready, right_late
    back = exchange(pack_back(own.astype(BF), *sides, experts), experts)
    grad_x = combine_rows(back, pick, experts, features)
    grads = weight_grads(
        (near_xm, far_xm, near_xt, far_xt), (near_m, far_m, near_t, far_t), (terms_nm, terms_fm, terms_nt, terms_ft), features
    )
    return (grad_x, *grads)


def solution(mesh):
    rows = P(("dp", "expert"), None)
    columns = P("expert", None, "dp")
    down = P("expert", "dp", None)
    return jax.shard_map(
        per_device,
        mesh=mesh,
        in_specs=(rows, rows, rows, rows, columns, columns, down),
        out_specs=(rows, columns, columns, down),
        check_vma=False,
    )
```

```python
import functools

import jax
import jax.numpy as jnp
from jax import lax
from jax.experimental import pallas as pl
from jax.experimental.pallas import tpu as pltpu
from jax.sharding import PartitionSpec as P


BF = jnp.bfloat16
F32 = jnp.float32
LANES = 128
SLOTS = 3


def held(a):
    return pltpu.with_memory_space_constraint(a, pltpu.VMEM)


def chunk_rows(tiles):
    return -(-SLOTS * tiles // 8) * 8


def deal(scratch, experts, tiles, value):
    chunk = chunk_rows(tiles)
    for j in range(SLOTS):
        for c in range(tiles):
            scratch[pl.ds(j * tiles + c, experts, stride=chunk), :] = value(
                slice(j * experts, (j + 1) * experts), slice(c * LANES, (c + 1) * LANES)
            )
    for n in range(SLOTS * tiles, chunk):
        scratch[pl.ds(n, experts, stride=chunk), :] = jnp.zeros((experts, LANES), F32)


def collect(scratch, experts, tiles, out):
    chunk = chunk_rows(tiles)
    for j in range(SLOTS):
        for c in range(tiles):
            out[j * experts : (j + 1) * experts, c * LANES : (c + 1) * LANES] = scratch[
                pl.ds(j * tiles + c, experts, stride=chunk), :
            ].astype(BF)


def pack_kernel(tok, cot, routes, gates, out_x, out_dy, pick, picked, scratch, *, experts):
    rows, features = tok.shape
    top = routes.shape[1]
    tiles = features // LANES
    lane = lax.broadcasted_iota(jnp.int32, (rows, LANES), 1)
    expert_of = lane % experts
    slot_of = lane // experts
    hit = jnp.zeros((rows, LANES), F32)
    gate = jnp.zeros((rows, LANES), F32)
    for k in range(top):
        same = routes[:, k : k + 1] == expert_of
        hit = jnp.where(same, 1.0, hit)
        gate = jnp.where(same, gates[:, k : k + 1].astype(F32), gate)
    below = lax.broadcasted_iota(jnp.int32, (rows, rows), 1) < lax.broadcasted_iota(jnp.int32, (rows, rows), 0)
    rank = jnp.dot(below.astype(BF), hit.astype(BF), preferred_element_type=F32)
    chosen = (hit > 0.5) & (rank == slot_of.astype(F32))
    sel = jnp.where(chosen, 1.0, 0.0)
    pick[...] = sel.astype(BF)

    def spread(mask, values):
        return lax.dot_general(mask.astype(BF), values, (((0,), (0,)), ((), ())), preferred_element_type=F32)

    picked[:, :features] = spread(sel, tok[...])
    deal(scratch, experts, tiles, lambda r, c: picked[r, c])
    out_x[...] = scratch[...].astype(BF)
    picked[:, :features] = spread(sel, cot[...])
    picked[:, features:] = spread(sel * gate, jnp.ones((rows, LANES), BF))
    deal(scratch, experts, tiles + 1, lambda r, c: picked[r, c])
    out_dy[...] = scratch[...].astype(BF)


def pack_rows(tokens, cotangent, routes, gates, experts):
    rows, features = tokens.shape
    tiles = features // LANES
    assert chunk_rows(tiles) == chunk_rows(tiles + 1)
    flat = (experts * chunk_rows(tiles), LANES)
    return pl.pallas_call(
        functools.partial(pack_kernel, experts=experts),
        out_shape=(
            jax.ShapeDtypeStruct(flat, BF),
            jax.ShapeDtypeStruct(flat, BF),
            jax.ShapeDtypeStruct((rows, LANES), BF),
        ),
        scratch_shapes=[pltpu.VMEM((LANES, features + LANES), F32), pltpu.VMEM(flat, F32)],
        name="pack_rows",
    )(tokens, cotangent, routes, gates)


def unpack_kernel(flat, out, scratch, *, experts):
    scratch[...] = flat[...].astype(F32)
    collect(scratch, experts, out.shape[1] // LANES, out)


def unpack_rows(flat, experts, width):
    return pl.pallas_call(
        functools.partial(unpack_kernel, experts=experts),
        out_shape=jax.ShapeDtypeStruct((SLOTS * experts, width), BF),
        scratch_shapes=[pltpu.VMEM(flat.shape, F32)],
        name="unpack_rows",
    )(held(flat))


def back_kernel(own, left_low, left_high, right_low, right_high, out, scratch, *, experts):
    half = own.shape[0] // 2

    def value(r, c):
        low, high = slice(r.start, min(r.stop, half)), slice(max(r.start, half) - half, r.stop - half)
        left, right = (
            jnp.concatenate([p[s, c] for p, s in ((a, low), (b, high)) if s.start < s.stop], axis=0).astype(F32)
            for a, b in ((left_low, left_high), (right_low, right_high))
        )
        return own[r, c].astype(F32) + left + right

    deal(scratch, experts, own.shape[1] // LANES, value)
    out[...] = scratch[...].astype(BF)


def pack_back(own, left_low, left_high, right_low, right_high, experts):
    flat = (experts * chunk_rows(own.shape[1] // LANES), LANES)
    return pl.pallas_call(
        functools.partial(back_kernel, experts=experts),
        out_shape=jax.ShapeDtypeStruct(flat, BF),
        scratch_shapes=[pltpu.VMEM(flat, F32)],
        name="pack_back",
    )(*(held(a) for a in (own, left_low, left_high, right_low, right_high)))


def combine_kernel(flat, pick, out, scratch, rows_ref, *, experts):
    scratch[...] = flat[...].astype(F32)
    collect(scratch, experts, out.shape[1] // LANES, rows_ref)
    out[...] = jnp.dot(pick[:, : SLOTS * experts], rows_ref[...], preferred_element_type=F32).astype(BF)


def combine_rows(flat, pick, experts, features):
    return pl.pallas_call(
        functools.partial(combine_kernel, experts=experts),
        out_shape=jax.ShapeDtypeStruct((pick.shape[0], features), BF),
        scratch_shapes=[pltpu.VMEM(flat.shape, F32), pltpu.VMEM((SLOTS * experts, features), BF)],
        name="combine_rows",
    )(held(flat), pick)


def weight_grads_kernel(*refs, xs, dys):
    refs = list(refs)
    take = lambda n: [refs.pop(0) for _ in range(n)]
    rows_x, rows_dy, hidden, d_gate, d_up = take(xs), take(dys), take(dys), take(dys), take(dys)
    out_gate, out_up, out_down = refs

    def product(a, b):
        a, b = (jnp.concatenate([piece[...] for piece in side], axis=0) for side in (a, b))
        return lax.dot_general(a, b, (((0,), (0,)), ((), ())), preferred_element_type=F32).astype(BF)

    out_gate[0] = product(rows_x, d_gate)
    out_up[0] = product(rows_x, d_up)
    out_down[0] = product(hidden, rows_dy)


def weight_grads(rows_x, rows_dy, terms, features):
    step = 512
    width = terms[0][0].shape[1]
    columns = tuple(zip(*terms))
    operands = [*rows_x, *rows_dy, *columns[0], *columns[1], *columns[2]]
    specs = [pl.BlockSpec((a.shape[0], step), lambda i: (0, i)) for a in (*rows_x, *rows_dy)]
    specs += [pl.BlockSpec(a.shape, lambda i: (0, 0)) for a in operands[len(specs) :]]
    tall = pl.BlockSpec((1, step, width), lambda i: (0, i, 0))
    return pl.pallas_call(
        functools.partial(weight_grads_kernel, xs=len(rows_x), dys=len(rows_dy)),
        grid=(features // step,),
        in_specs=specs,
        out_specs=(tall, tall, pl.BlockSpec((1, width, step), lambda i: (0, 0, i))),
        out_shape=(
            jax.ShapeDtypeStruct((1, features, width), BF),
            jax.ShapeDtypeStruct((1, features, width), BF),
            jax.ShapeDtypeStruct((1, width, features), BF),
        ),
        name="weight_grads",
    )(*operands)


def exchange(flat, experts):
    chunks = flat.reshape(experts, -1, LANES)
    out = lax.all_to_all(chunks, "expert", split_axis=0, concat_axis=0, tiled=True)
    return out.reshape(-1, LANES)


def shift(a, by, size):
    return lax.ppermute(a, "dp", [(i, (i + 2 * by) % size) for i in range(size)])


def swap(a, size):
    return lax.ppermute(a, "dp", [(i, i ^ 1) for i in range(size)])


def after(values, *others):
    return lax.optimization_barrier((tuple(values), others))[0] if others else tuple(values)


def projections(rows, gate_mat, up_mat):
    gate_pre = jnp.dot(rows, gate_mat, preferred_element_type=F32)
    up_pre = jnp.dot(rows, up_mat, preferred_element_type=F32)
    return gate_pre, up_pre


def expert_terms(rows, gate_pre, up_pre, gate_mat, up_mat, down_mat):
    features = gate_mat.shape[0]
    weight = rows[:, features : features + 1].astype(F32)
    sig = jax.nn.sigmoid(gate_pre)
    activated = gate_pre * sig
    hidden = (weight * activated * up_pre).astype(BF)
    returned = weight * jnp.dot(rows[:, :features], down_mat.T, preferred_element_type=F32)
    d_gate = (returned * up_pre * sig * (1.0 + gate_pre * (1.0 - sig))).astype(BF)
    d_up = (returned * activated).astype(BF)
    total = jnp.dot(d_gate, gate_mat.T, preferred_element_type=F32) + jnp.dot(
        d_up, up_mat.T, preferred_element_type=F32
    )
    return total, (hidden, d_gate, d_up)


def per_device(tokens, cotangent, routes, gates, w_gate, w_up, w_down):
    features = tokens.shape[1]
    experts = lax.axis_size("expert")
    size = lax.axis_size("dp")
    mats = w_gate[0], w_up[0], w_down[0]
    flat_x, flat_dy, pick = pack_rows(tokens, cotangent, routes, gates, experts)
    own_x = unpack_rows(exchange(flat_x, experts), experts, features)
    rows = own_x.shape[0]
    half = rows // 2
    behind, ahead = shift(own_x, 1, size), shift(own_x, -1, size)
    halves = behind[:half], ahead[half:]
    far = shift(halves[0], 1, size), shift(halves[1], -1, size)
    (flat_dy,) = after((exchange(flat_dy, experts),), *halves)
    own_dy = unpack_rows(flat_dy, experts, features + LANES)
    early = shift(own_dy[:half], 1, size), shift(own_dy[half:], -1, size)
    near_xm = jnp.concatenate(after((own_x, *halves, behind[half:], ahead[:half]), own_dy), axis=0)
    near_xt = swap(near_xm, size)
    pre_nm = projections(near_xm, *mats[:2])
    far_xm = jnp.concatenate(after(far, *pre_nm), axis=0)
    far_x = jnp.concatenate((far_xm, swap(far_xm, size)), axis=0)
    early = after(early, far_x)
    far = shift(early[0], 1, size), shift(early[1], -1, size)
    pre_nt = projections(near_xt, *mats[:2])
    pre_f = projections(far_x, *mats[:2])
    soon = 2 * rows
    early_m = jnp.concatenate(after((own_dy, *early), *pre_nt, *pre_f), axis=0)
    early_t = swap(early_m, size)
    late = after((own_dy[half:], own_dy[:half]), early_t)
    late = shift(late[0], 1, size), shift(late[1], -1, size)
    total_et, terms_et = expert_terms(early_t, *(a[:soon] for a in pre_nt), *mats)
    total_et = total_et.astype(BF)
    total_em, terms_em = expert_terms(*after((early_m,), total_et), *(a[:soon] for a in pre_nm), *mats)
    total_e = total_em + swap(total_et, size).astype(F32)
    far_m = jnp.concatenate(after(far, total_em), axis=0)
    far_t = swap(far_m, size)
    own = total_e[:rows]
    right_ready = shift(total_e[rows : rows + half].astype(BF), -1, size)
    left_ready = shift(total_e[rows + half :].astype(BF), 1, size)
    far_dy = jnp.concatenate((far_m, far_t), axis=0)
    total_f, terms_f = expert_terms(far_dy, *pre_f, *mats)
    across = (total_f[:rows] + swap(total_f[rows:].astype(BF), size).astype(F32)).astype(BF)
    from_behind = shift(across[:half], 1, size).astype(F32)
    from_ahead = shift(across[half:], -1, size).astype(F32)
    late_m = jnp.concatenate(after(late, total_f), axis=0)
    late_t = swap(late_m, size)
    late_dy = jnp.concatenate(after((late_m, late_t), across), axis=0)
    pre_l = (jnp.concatenate((m[soon:], t[soon:]), axis=0) for m, t in zip(pre_nm, pre_nt))
    total_l, terms_l = expert_terms(late_dy, *pre_l, *mats)
    total_l = total_l[:rows] + swap(total_l[rows:].astype(BF), size).astype(F32)
    right_late = shift((total_l[:half] + from_ahead).astype(BF), -1, size)
    left_late = shift((total_l[half:] + from_behind).astype(BF), 1, size)
    sides = left_late, left_ready, right_ready, right_late
    back = exchange(pack_back(own.astype(BF), *sides, experts), experts)
    grad_x = combine_rows(back, pick, experts, features)
    terms_lm, terms_lt = tuple(a[:rows] for a in terms_l), tuple(a[rows:] for a in terms_l)
    grads = weight_grads(
        (near_xm, near_xt, far_x),
        (early_m, late_m, early_t, late_t, far_dy),
        (terms_em, terms_lm, terms_et, terms_lt, terms_f),
        features,
    )
    return (grad_x, *grads)


def solution(mesh):
    rows = P(("dp", "expert"), None)
    columns = P("expert", None, "dp")
    down = P("expert", "dp", None)
    return jax.shard_map(
        per_device,
        mesh=mesh,
        in_specs=(rows, rows, rows, rows, columns, columns, down),
        out_specs=(rows, columns, columns, down),
        check_vma=False,
    )
```
